512 devices in a mesh: row: 8 (over x, y_hi), blk: 64 (over y_lo, z, core).
Axes of the slice: x: 4, y: 8 (y_hi: 2, y_lo: 4; y = y_hi * 4 + y_lo), z: 8, core: 2. Of those that a mesh axis runs over, the one named last changes fastest.
Arguments:
- matrix: float32 [16384, 8192], P('row', 'blk'), may hold values from -72 to 72, as said below
- prior: float32 [8192, 8192], P('row', 'blk'), may hold values from -6 to 6
Outputs:
- turned: float32 [16384, 8192], P('row', 'blk')
- transform: float32 [8192, 8192], P('row', 'blk')
- off_ratio: float32 [8], replicated
The draws below stay inside these ranges and needn't reach their ends.
Inputs may be any that keep to these rules, and one draw needn't show every extreme that they name: `matrix`: every column is nonzero.
All inputs are finite; a program needn't handle non-finite values.
Results may differ from the reference program's by a relative error of at most 0.0003.
Values sent between devices are 32-bit elements; how exact they have to be, the bound alone decides.
No kernel may reach another device: no remote copies, remote signals or barrier semaphores. Data moves between devices by JAX's collectives and lax.ppermute only.
A program may use at most 64 MiB of HBM per device.

```python
import jax
import jax.numpy as jnp
from jax import lax

ROUNDS = 8
NS_STEPS = 8
ROWS = 16384
COLS = 8192
N_BLK = 64


def draw_matrix(key, part):
    keys = jax.random.split(key, 5)
    noise = jnp.clip(jax.random.normal(keys[0], (ROWS, COLS), jnp.float32), -6.0, 6.0)
    strength = 0.6
    common_rows = jnp.clip(jax.random.normal(keys[1], (ROWS, 1), jnp.float32), -6.0, 6.0)
    common_cols = jax.random.uniform(keys[2], (1, COLS), jnp.float32, -1.0, 1.0)
    row_scale = jnp.exp(jax.random.uniform(keys[3], (ROWS, 1), jnp.float32, jnp.log(0.3), jnp.log(3.0)))
    position = jnp.arange(COLS, dtype=jnp.float32)[None, :] / COLS
    col_scale = jnp.exp(jax.random.uniform(keys[4], (1, COLS), jnp.float32, jnp.log(0.5), jnp.log(2.0))) * jnp.exp(-1.2 * position)
    return row_scale * col_scale * (noise + strength * common_rows * common_cols)


def block_scale(stream_key, extent, pieces, least, top_value):
    def one(dim, parts):
        draws = jax.random.uniform(jax.random.fold_in(jax.random.fold_in(stream_key, 6), dim), (parts,), jnp.float32, least / len(pieces), top_value / len(pieces))
        return jnp.repeat(jnp.exp(draws), extent[dim] // parts).reshape((-1,) + (1,) * (len(extent) - dim - 1))

    gain = one(*pieces[0])
    for cut in pieces[1:]:
        gain = gain * one(*cut)
    return gain


def gaussian(own_key, extent, spread, limit, cuts=(), kind=jnp.bfloat16):
    gain = block_scale(own_key, extent, cuts, -0.22, 0.18) if cuts else 1.0
    values = jax.random.normal(own_key, extent, jnp.float32) * spread * gain
    return jnp.minimum(jnp.maximum(values, -limit), limit).astype(kind)


def setup_inputs(seed: int = 0) -> dict:
    arg_keys = jax.random.split(jax.random.key(seed), 3)
    return {
        "matrix": draw_matrix(jax.random.fold_in(arg_keys[2], 71), 0),
        "prior": gaussian(arg_keys[1], (COLS, COLS), 1.0, 6.0, ((0, 8), (1, 64)), jnp.float32),
    }


HIGH = lax.Precision.HIGHEST

def rotation(gram_sum):
    pair_width = gram_sum.shape[0]
    diag_vals = jnp.diagonal(gram_sum)
    weights = jnp.arange(pair_width, dtype=jnp.float32) / pair_width
    mean_diag = jnp.mean(diag_vals)
    skew_part = gram_sum * (weights[None, :] - weights[:, None]) / mean_diag
    factor = lax.rsqrt(1.0 + jnp.sum(skew_part * skew_part))
    identity = jnp.eye(pair_width, dtype=jnp.float32)
    rotator = (identity + skew_part) * factor
    for repeat in range(NS_STEPS):
        square = jnp.dot(rotator.T, rotator, precision=HIGH, preferred_element_type=jnp.float32)
        rotator = 1.5 * rotator - 0.5 * jnp.dot(rotator, square, precision=HIGH, preferred_element_type=jnp.float32)
    off_sq = jnp.sum(jnp.where(identity > 0.5, 0.0, gram_sum * gram_sum))
    diag_sq = jnp.sum(diag_vals * diag_vals)
    return (rotator, off_sq, diag_sq)

def reference(matrix, prior):
    row_count, col_count = matrix.shape
    blocks = N_BLK
    pair_width = col_count // blocks
    half_width = pair_width // 2
    frames = matrix.reshape(row_count, blocks, pair_width).transpose(1, 0, 2)
    earlier = prior.reshape(col_count, blocks, pair_width).transpose(1, 0, 2)
    frames = jnp.concatenate([frames, earlier], axis=1)

    def turn_pair(stacked):
        local_rows = stacked[:row_count]
        gram_sum = jnp.dot(local_rows.T, local_rows, precision=HIGH, preferred_element_type=jnp.float32)
        rotator, off_sq, diag_sq = rotation(gram_sum)
        return (jnp.dot(stacked, rotator, precision=HIGH, preferred_element_type=jnp.float32), off_sq, diag_sq)
    history = []
    for round_index in range(ROUNDS):
        frames, off_all, diag_all = lax.map(turn_pair, frames)
        history.append(jnp.sqrt(jnp.sum(off_all) / jnp.sum(diag_all)))
        top_turned = frames[:, :, :half_width]
        bottom_turned = frames[:, :, half_width:]
        new_top = jnp.concatenate([top_turned[:1], bottom_turned[:1], top_turned[1:blocks - 1]], axis=0)
        new_bottom = jnp.concatenate([bottom_turned[1:], top_turned[blocks - 1:]], axis=0)
        frames = jnp.concatenate([new_top, new_bottom], axis=2)
    result = frames.transpose(1, 0, 2).reshape(row_count + col_count, col_count)
    return (result[:row_count], result[row_count:], jnp.stack(history))
```

```python
import functools

import jax
import jax.numpy as jnp
from jax import lax
from jax.experimental import pallas as pl
from jax.experimental.pallas import tpu as pltpu
from jax.sharding import PartitionSpec as P

ROUNDS = 8
NS_STEPS = 8
W = 128
H = 64
F32 = jnp.float32
BF16 = jnp.bfloat16


def split(x):
    hi = x.astype(BF16)
    return hi, (x - hi.astype(F32)).astype(BF16)


def dot(a, b):
    return jnp.dot(a, b, preferred_element_type=F32)


def dot_t(a, b):
    return lax.dot_general(a, b, (((0,), (0,)), ((), ())), preferred_element_type=F32)


def matmul(a, b):
    ah, al = split(a)
    bh, bl = split(b)
    return dot(ah, bh) + (dot(ah, bl) + dot(al, bh))


def lanes(shape):
    return lax.broadcasted_iota(jnp.int32, shape, len(shape) - 1)


def rows(shape):
    return lax.broadcasted_iota(jnp.int32, shape, 0)


def swap(x):
    return pltpu.roll(x, H, 1)


def fold(m):
    s = swap(m)
    return jnp.where(lanes((32, W)) < H, m[:32] + s[64:96], s[32:64] + m[96:128])


def blocks(m):
    s = swap(m)
    left = lanes((32, W)) < H
    return jnp.where(left, m[:32], s[32:64]), jnp.where(left, s[64:96], m[96:128])


def cross(z, d):
    zh, zl = split(z)
    dh, dl = split(d)
    m = dot_t(jnp.concatenate([zh, zl], 1), jnp.concatenate([dh, dl], 1))
    return (m[:W, :W] + m[W:, W:]) + (m[:W, W:] + m[W:, :W])


def spread(r, first):
    r = jnp.where(first, r, swap(r))
    s = swap(r)
    left = lanes((H, W)) < H
    out = []
    for k in (0, H):
        u, v = r[k : k + H], s[k : k + H]
        out.append(jnp.concatenate([jnp.where(left, u, 0.0), jnp.where(left, v, 0.0)], 1))
        out.append(jnp.concatenate([jnp.where(left, 0.0, v), jnp.where(left, 0.0, u)], 1))
    return jnp.concatenate(out, 0)


def apply(wh, wl, z, d):
    x = jnp.concatenate([z, d], 1)
    xh, xl = split(x)
    return dot(xh, wh) + (dot(xh, wl) + dot(xl, wh))


def pack_kernel(flag, x_ref, p_ref, az, ad, pz, pd, part):
    odd = flag[0] == 1
    for ref, z_ref, d_ref in ((x_ref, az, ad), (p_ref, pz, pd)):
        h = ref.shape[0] // 2
        lo, hi = ref[:h], ref[h:]
        left = lanes((h, W)) < H
        top = jnp.where(left, lo, swap(hi))
        bottom = jnp.where(left, swap(lo), hi)
        z_ref[:h] = jnp.where(odd, bottom, top)
        d_ref[:h] = jnp.where(odd, top, bottom)
    pz[p_ref.shape[0] // 2 :] = jnp.zeros((32, W), F32)
    pd[p_ref.shape[0] // 2 :] = jnp.zeros((32, W), F32)
    z, d = az[...], ad[...]
    both = jnp.concatenate([fold(cross(z, d)), fold(cross(z, z)), fold(cross(d, d))], 0)
    for k in range(8):
        part[k] = both


def rotator_of(flag, n, ez, ed, rnd, stat, stat_out):
    left = lanes((H, W)) < H
    upper = jnp.where(
        left, jnp.concatenate([ez, swap(ez)], 0) * 0.5, jnp.concatenate([swap(n), n], 0)
    )
    lower = jnp.where(left, 0.0, jnp.concatenate([swap(ed), ed], 0) * 0.5)
    half = jnp.concatenate([upper, lower], 0)
    gram = half + half.T
    i, j = rows((W, W)), lanes((W, W))
    odd = flag[0] == 1
    step = jnp.where(odd, ((j + H) % W) - ((i + H) % W), j - i).astype(F32) * (1.0 / W)
    eye = i == j
    diag = jnp.where(eye, gram, 0.0)
    mean = jnp.sum(diag) * (1.0 / W)
    skew = gram * step / mean
    factor = lax.rsqrt(jnp.full((1, 1), 1.0, F32) + jnp.sum(skew * skew))
    one = jnp.where(eye, 1.0, 0.0)
    x = (one + skew) * factor
    y = (one - matmul(skew, skew)) * (factor * factor)
    for k in range(NS_STEPS):
        w = 1.5 * one - 0.5 * y
        wh, wl = split(w)
        if k + 1 < NS_STEPS:
            xh, xl = split(jnp.concatenate([x, y], 0))
            v = dot(xh, wh) + (dot(xh, wl) + dot(xl, wh))
            x = v[:W]
            vh, vl = split(v[W:])
            y = dot(vh, wh) + (dot(vh, wl) + dot(vl, wh))
        else:
            x = matmul(x, w)
    off = jnp.sum(jnp.where(eye, 0.0, gram * gram))
    dsq = jnp.sum(diag * diag)
    lane = lanes((8, W))
    stat_out[...] = jnp.where(lane == rnd, off, jnp.where(lane == rnd + 8, dsq, stat[...]))
    return x, gram


def turn_kernel(rnd, flag, part, ez_ref, ed_ref, stat, az, ad, az_out, ad_out, r_out, g_out, stat_out):
    total = ((part[0] + part[1]) + (part[2] + part[3])) + ((part[4] + part[5]) + (part[6] + part[7]))
    if rnd == 0:
        n, ez, ed = total[:32], total[32:64], total[64:96]
    else:
        n, ez, ed = total, ez_ref[ez_ref.shape[0] - 32 :], ed_ref[ed_ref.shape[0] - 32 :]
    r, gram = rotator_of(flag, n, ez, ed, rnd, stat, stat_out)
    r_out[...] = r
    g_out[...] = gram
    wh, wl = split(spread(r, flag[1] == 1))
    count = az.shape[0]
    chunk = 256
    for k in range(0, count, chunk):
        o = apply(wh, wl, az[k : k + chunk], ad[k : k + chunk])
        az_out[k : k + chunk] = o[:, :W]
        ad_out[k : k + chunk] = o[:, W:]


def prior_kernel(flag, r_ref, g_ref, pz, pd, pz_out, pd_out):
    r = r_ref[...]
    first = flag[1] == 1
    wh, wl = split(spread(r, first))
    count = pz.shape[0] - 32
    chunk = 256
    for k in range(0, count, chunk):
        o = apply(wh, wl, pz[k : k + chunk], pd[k : k + chunk])
        pz_out[k : k + chunk] = o[:, :W]
        pd_out[k : k + chunk] = o[:, W:]
    rs = jnp.where(first, r, swap(r))
    e = matmul(rs.T, matmul(g_ref[...], rs))
    ez, ed = blocks(e)
    pz_out[count:] = ez
    pd_out[count:] = ed


def gram_kernel(az, ad, part):
    n = fold(cross(az[...], ad[...]))
    for k in range(8):
        part[k] = n


def unpack_kernel(flag, az, ad, pz, pd, x_ref, p_ref):
    odd = flag[0] == 1
    for ref, z_ref, d_ref in ((x_ref, az, ad), (p_ref, pz, pd)):
        h = ref.shape[0] // 2
        z, d = z_ref[:h], d_ref[:h]
        top = jnp.where(odd, d, z)
        bottom = jnp.where(odd, z, d)
        left = lanes((h, W)) < H
        ref[:h] = jnp.where(left, top, swap(bottom))
        ref[h:] = jnp.where(left, swap(top), bottom)


VMEM = pl.BlockSpec(memory_space=pltpu.VMEM)
SMEM = pl.BlockSpec(memory_space=pltpu.SMEM)


def call(kernel, outs, specs, flops=0):
    return pl.pallas_call(
        kernel,
        out_shape=tuple(jax.ShapeDtypeStruct(s, F32) for s in outs),
        in_specs=specs,
        out_specs=tuple(VMEM for _ in outs),
        cost_estimate=pl.CostEstimate(flops=flops, bytes_accessed=1 << 20, transcendentals=0),
        compiler_params=pltpu.CompilerParams(vmem_limit_bytes=16 << 20),
    )


def body(matrix, prior):
    ra, rp = matrix.shape[0] // 2, prior.shape[0] // 2
    blk_count = lax.axis_size("blk")
    slot = lax.axis_index("blk")
    flag = jnp.stack([slot % 2, (slot == 0).astype(jnp.int32)]).astype(jnp.int32)
    last = blk_count - 1
    over_z = [(0, 0), (last, last)]
    for i in range(1, last, 2):
        over_z += [(i, i + 1), (i + 1, i)]
    over_d = []
    for i in range(0, last, 2):
        over_d += [(i, i + 1), (i + 1, i)]
    e = rp + 32
    az, ad, pz, pd, part = call(
        pack_kernel, [(ra, W), (ra, W), (e, W), (e, W), (8, 96, W)], [SMEM, VMEM, VMEM], 1 << 30
    )(flag, matrix, prior)
    stat = jnp.zeros((8, W), F32)
    for rnd in range(ROUNDS):
        part = lax.all_to_all(part, "row", 0, 0)
        az, ad, r, g, stat = call(
            functools.partial(turn_kernel, rnd),
            [(ra, W), (ra, W), (W, W), (W, W), (8, W)],
            [SMEM, VMEM, VMEM, VMEM, VMEM, VMEM, VMEM],
            1 << 30,
        )(flag, part, pz, pd, stat, az, ad)
        az = lax.ppermute(az, "blk", over_z)
        ad = lax.ppermute(ad, "blk", over_d)
        pz, pd = call(
            prior_kernel, [(e, W), (e, W)], [SMEM, VMEM, VMEM, VMEM, VMEM], 1 << 28
        )(flag, r, g, pz, pd)
        pz = lax.ppermute(pz, "blk", over_z)
        pd = lax.ppermute(pd, "blk", over_d)
        if rnd + 1 < ROUNDS:
            (part,) = call(gram_kernel, [(8, 32, W)], [VMEM, VMEM], 1 << 28)(az, ad)
    turned, transform = call(
        unpack_kernel, [matrix.shape, prior.shape], [SMEM, VMEM, VMEM, VMEM, VMEM]
    )(flag, az, ad, pz, pd)
    rows_of = jnp.broadcast_to(stat[None, :1], (blk_count, 1, W))
    total = jnp.sum(lax.all_to_all(rows_of, "blk", 0, 0), axis=(0, 1))
    off_ratio = jnp.sqrt(total[:ROUNDS] / total[8 : 8 + ROUNDS])
    return turned, transform, off_ratio


def solution(mesh):
    return jax.shard_map(
        body,
        mesh=mesh,
        in_specs=(P("row", "blk"), P("row", "blk")),
        out_specs=(P("row", "blk"), P("row", "blk"), P()),
        check_vma=False,
    )
```

```python
import functools

import jax
import jax.numpy as jnp
from jax import lax
from jax.experimental import pallas as pl
from jax.experimental.pallas import tpu as pltpu
from jax.sharding import PartitionSpec as P

ROUNDS = 8
NS_STEPS = 8
W = 128
H = 64
F32 = jnp.float32
BF16 = jnp.bfloat16


def split(x):
    hi = x.astype(BF16)
    return hi, (x - hi.astype(F32)).astype(BF16)


def dot(a, b):
    return jnp.dot(a, b, preferred_element_type=F32)


def dot_t(a, b):
    return lax.dot_general(a, b, (((0,), (0,)), ((), ())), preferred_element_type=F32)


def matmul(a, b):
    ah, al = split(a)
    bh, bl = split(b)
    b = jnp.concatenate([bh, bl], 1)
    m = dot(jnp.concatenate([ah, al], 1), jnp.concatenate([b, b], 0))
    return m[:, :W] + m[:, W:]


def lanes(shape):
    return lax.broadcasted_iota(jnp.int32, shape, len(shape) - 1)


def rows(shape):
    return lax.broadcasted_iota(jnp.int32, shape, 0)


def swap(x):
    return pltpu.roll(x, H, 1)


def fold(m):
    s = swap(m)
    return jnp.where(lanes((32, W)) < H, m[:32] + s[64:96], s[32:64] + m[96:128])


def blocks(m):
    s = swap(m)
    left = lanes((32, W)) < H
    return jnp.where(left, m[:32], s[32:64]), jnp.where(left, s[64:96], m[96:128])


def cross(z, d):
    zh, zl = split(z)
    dh, dl = split(d)
    m = dot_t(jnp.concatenate([zh, zl], 1), jnp.concatenate([dh, dl], 1))
    return (m[:W, :W] + m[W:, W:]) + (m[:W, W:] + m[W:, :W])


def spread(r, first):
    r = jnp.where(first, r, swap(r))
    s = swap(r)
    left = lanes((H, W)) < H
    out = []
    for k in (0, H):
        u, v = r[k : k + H], s[k : k + H]
        out.append(jnp.concatenate([jnp.where(left, u, 0.0), jnp.where(left, v, 0.0)], 1))
        out.append(jnp.concatenate([jnp.where(left, 0.0, v), jnp.where(left, 0.0, u)], 1))
    return jnp.concatenate(out, 0)


def apply(wh, wl, z, d):
    x = jnp.concatenate([z, d], 1)
    xh, xl = split(x)
    return dot(xh, wh) + (dot(xh, wl) + dot(xl, wh))


def pack_kernel(flag, x_ref, p_ref, az, ad, pz, pd, part):
    odd = flag[0] == 1
    for ref, z_ref, d_ref in ((x_ref, az, ad), (p_ref, pz, pd)):
        h = ref.shape[0] // 2
        lo, hi = ref[:h], ref[h:]
        left = lanes((h, W)) < H
        top = jnp.where(left, lo, swap(hi))
        bottom = jnp.where(left, swap(lo), hi)
        z_ref[:h] = jnp.where(odd, bottom, top)
        d_ref[:h] = jnp.where(odd, top, bottom)
    pz[p_ref.shape[0] // 2 :] = jnp.zeros((32, W), F32)
    pd[p_ref.shape[0] // 2 :] = jnp.zeros((32, W), F32)
    z, d = az[...], ad[...]
    both = jnp.concatenate([fold(cross(z, d)), fold(cross(z, z)), fold(cross(d, d))], 0)
    for k in range(8):
        part[k] = both


def rotator_of(flag, n, ez, ed):
    left = lanes((H, W)) < H
    upper = jnp.where(
        left, jnp.concatenate([ez, swap(ez)], 0) * 0.5, jnp.concatenate([swap(n), n], 0)
    )
    lower = jnp.where(left, 0.0, jnp.concatenate([swap(ed), ed], 0) * 0.5)
    half = jnp.concatenate([upper, lower], 0)
    gram = half + half.T
    i, j = rows((W, W)), lanes((W, W))
    odd = flag[0] == 1
    step = jnp.where(odd, ((j + H) % W) - ((i + H) % W), j - i).astype(F32) * (1.0 / W)
    eye = i == j
    mean = jnp.sum(jnp.where(eye, gram, 0.0)) * (1.0 / W)
    skew = gram * step / mean
    factor = lax.rsqrt(jnp.full((1, 1), 1.0, F32) + jnp.sum(skew * skew))
    one = jnp.where(eye, 1.0, 0.0)
    x = (one + skew) * factor
    y = (one - matmul(skew, skew)) * (factor * factor)
    for k in range(NS_STEPS - 1):
        w = 1.5 * one - 0.5 * y
        if k + 2 < NS_STEPS:
            y = matmul(matmul(y, w), w)
        x = matmul(x, w)
    return 1.5 * x - 0.5 * matmul(x, matmul(x.T, x)), gram


def stats_of(gram, rnd, stat):
    eye = rows((W, W)) == lanes((W, W))
    square = gram * gram
    off = jnp.sum(jnp.where(eye, 0.0, square))
    dsq = jnp.sum(jnp.where(eye, square, 0.0))
    lane = lanes((8, W))
    return jnp.where(lane == rnd, off, jnp.where(lane == rnd + 8, dsq, stat))


def turn_kernel(rnd, flag, part, ez_ref, ed_ref, az, ad, stat, az_out, ad_out, r_out, g_out, stat_out):
    total = ((part[0] + part[1]) + (part[2] + part[3])) + ((part[4] + part[5]) + (part[6] + part[7]))
    if rnd == 0:
        n, ez, ed = total[:32], total[32:64], total[64:96]
    else:
        n, ez, ed = total, ez_ref[ez_ref.shape[0] - 32 :], ed_ref[ed_ref.shape[0] - 32 :]
    r, gram = rotator_of(flag, n, ez, ed)
    r_out[...] = r
    g_out[...] = gram
    stat_out[...] = stats_of(gram, rnd, stat[...]) if rnd + 1 == ROUNDS else stat[...]
    wh, wl = split(spread(r, flag[1] == 1))
    count = az.shape[0]
    chunk = 256
    for k in range(0, count, chunk):
        o = apply(wh, wl, az[k : k + chunk], ad[k : k + chunk])
        az_out[k : k + chunk] = o[:, :W]
        ad_out[k : k + chunk] = o[:, W:]


def prior_kernel(rnd, flag, r_ref, g_ref, stat, pz, pd, pz_out, pd_out, stat_out):
    stat_out[...] = stat[...] if rnd + 1 == ROUNDS else stats_of(g_ref[...], rnd, stat[...])
    r = r_ref[...]
    first = flag[1] == 1
    wh, wl = split(spread(r, first))
    count = pz.shape[0] - 32
    chunk = 256
    for k in range(0, count, chunk):
        o = apply(wh, wl, pz[k : k + chunk], pd[k : k + chunk])
        pz_out[k : k + chunk] = o[:, :W]
        pd_out[k : k + chunk] = o[:, W:]
    rs = jnp.where(first, r, swap(r))
    e = matmul(rs.T, matmul(g_ref[...], rs))
    ez, ed = blocks(e)
    pz_out[count:] = ez
    pd_out[count:] = ed


def gram_kernel(az, ad, part):
    n = fold(cross(az[...], ad[...]))
    for k in range(8):
        part[k] = n


def unpack_kernel(flag, az, ad, pz, pd, x_ref, p_ref):
    odd = flag[0] == 1
    for ref, z_ref, d_ref in ((x_ref, az, ad), (p_ref, pz, pd)):
        h = ref.shape[0] // 2
        z, d = z_ref[:h], d_ref[:h]
        top = jnp.where(odd, d, z)
        bottom = jnp.where(odd, z, d)
        left = lanes((h, W)) < H
        ref[:h] = jnp.where(left, top, swap(bottom))
        ref[h:] = jnp.where(left, swap(top), bottom)


VMEM = pl.BlockSpec(memory_space=pltpu.VMEM)
SMEM = pl.BlockSpec(memory_space=pltpu.SMEM)


def call(kernel, outs, specs, flops=0):
    return pl.pallas_call(
        kernel,
        out_shape=tuple(jax.ShapeDtypeStruct(s, F32) for s in outs),
        in_specs=specs,
        out_specs=tuple(VMEM for _ in outs),
        cost_estimate=pl.CostEstimate(flops=flops, bytes_accessed=1 << 20, transcendentals=0),
        compiler_params=pltpu.CompilerParams(vmem_limit_bytes=16 << 20),
    )


def body(matrix, prior):
    ra, rp = matrix.shape[0] // 2, prior.shape[0] // 2
    blk_count = lax.axis_size("blk")
    slot = lax.axis_index("blk")
    flag = jnp.stack([slot % 2, (slot == 0).astype(jnp.int32)]).astype(jnp.int32)
    last = blk_count - 1
    over_z = [(0, 0), (last, last)]
    for i in range(1, last, 2):
        over_z += [(i, i + 1), (i + 1, i)]
    over_d = []
    for i in range(0, last, 2):
        over_d += [(i, i + 1), (i + 1, i)]
    e = rp + 32
    az, ad, pz, pd, part = call(
        pack_kernel, [(ra, W), (ra, W), (e, W), (e, W), (8, 96, W)], [SMEM, VMEM, VMEM], 1 << 30
    )(flag, matrix, prior)
    stat = jnp.zeros((8, W), F32)
    for rnd in range(ROUNDS):
        part = lax.all_to_all(part, "row", 0, 0)
        az, ad, r, g, stat = call(
            functools.partial(turn_kernel, rnd),
            [(ra, W), (ra, W), (W, W), (W, W), (8, W)],
            [SMEM, VMEM, VMEM, VMEM, VMEM, VMEM, VMEM],
            1 << 30,
        )(flag, part, pz, pd, az, ad, stat)
        if rnd + 1 == ROUNDS:
            stats = jnp.broadcast_to(stat[None, :1], (blk_count, 1, W))
            stats = lax.all_to_all(stats, "blk", 0, 0)
        az = lax.ppermute(az, "blk", over_z)
        ad = lax.ppermute(ad, "blk", over_d)
        pz, pd, stat = call(
            functools.partial(prior_kernel, rnd),
            [(e, W), (e, W), (8, W)],
            [SMEM, VMEM, VMEM, VMEM, VMEM, VMEM],
            1 << 28,
        )(flag, r, g, stat, pz, pd)
        pz = lax.ppermute(pz, "blk", over_z)
        pd = lax.ppermute(pd, "blk", over_d)
        if rnd + 1 < ROUNDS:
            (part,) = call(gram_kernel, [(8, 32, W)], [VMEM, VMEM], 1 << 28)(az, ad)
    turned, transform = call(
        unpack_kernel, [matrix.shape, prior.shape], [SMEM, VMEM, VMEM, VMEM, VMEM]
    )(flag, az, ad, pz, pd)
    total = jnp.sum(stats, axis=(0, 1))
    off_ratio = jnp.sqrt(total[:ROUNDS] / total[8 : 8 + ROUNDS])
    return turned, transform, off_ratio


def solution(mesh):
    return jax.shard_map(
        body,
        mesh=mesh,
        in_specs=(P("row", "blk"), P("row", "blk")),
        out_specs=(P("row", "blk"), P("row", "blk"), P()),
        check_vma=False,
    )
```
